32 devices in a mesh: shards: 2 (over core), tensor: 4 (over y, x), sections: 4 (over z).
Axes of the slice: x: 2, y: 2, z: 4, core: 2. Of those that a mesh axis runs over, the one named last changes fastest.
Arguments:
- weight: float32 [4, 1024, 1024], P('sections', None, 'tensor'), may hold values from -0.1875 to 0.1875
- basis: float32 [4, 1024, 256], P('sections'), may hold values from -0.1875 to 0.1875
- inputs: bfloat16 [4, 512, 1024], P('sections', 'shards'), may hold values from -6 to 6
- out_grads: bfloat16 [4, 512, 1024], P('sections', 'shards', 'tensor'), may hold values from -0.25 to 0.25
- first_moment: float32 [4, 256, 1024], P('sections', 'shards', 'tensor'), may hold values from -6 to 6
- second_moment: float32 [4, 256, 1024], P('sections', 'shards', 'tensor'), may hold values from 0.01 to 1
Outputs:
- new_weight: float32 [4, 1024, 1024], P('sections', None, 'tensor')
- new_basis: float32 [4, 1024, 256], P('sections')
- new_first: float32 [4, 256, 1024], P('sections', 'shards', 'tensor')
- new_second: float32 [4, 256, 1024], P('sections', 'shards', 'tensor')
The draws below stay inside these ranges and needn't reach their ends.
All inputs are finite; a program needn't handle non-finite values.
Results may differ from the reference program's by a relative error of at most 0.0003.
Values sent between devices are 32-bit elements; how exact they have to be, the bound alone decides.
No kernel may reach another device: no remote copies, remote signals or barrier semaphores. Data moves between devices by JAX's collectives and lax.ppermute only.
A program may use at most 64 MiB of HBM per device.

```python
import math
import jax
import jax.numpy as jnp
from jax import lax

D = 1024
F = 1024
R = 256
ITERS = 5
TOKENS = 512
LAYERS = 4


def steps_of(key, dims, pieces, low, largest):
    def one(position, parts):
        steps = jax.random.uniform(jax.random.fold_in(jax.random.fold_in(key, 6), position), (parts,), jnp.float32, low / len(pieces), largest / len(pieces))
        return jnp.repeat(jnp.exp(steps), dims[position] // parts).reshape((-1,) + (1,) * (len(dims) - position - 1))

    gain = one(*pieces[0])
    for cut in pieces[1:]:
        gain = gain * one(*cut)
    return gain


def gaussian(rng, dims, deviation, limit, pieces=(), held_as=jnp.bfloat16):
    result = jax.random.normal(rng, dims, jnp.float32) * deviation
    if len(pieces) > 0:
        result = steps_of(rng, dims, pieces, -0.22, 0.18) * result
    return jnp.clip(result, min=-limit, max=limit).astype(held_as)


def setup_inputs(seed: int = 0) -> dict:
    key_list = jax.random.split(jax.random.key(seed), 7)
    return {
        "weight": gaussian(key_list[0], (LAYERS, D, F), D ** -0.5, 0.1875, ((0, 4), (2, 4)), jnp.float32),
        "basis": gaussian(key_list[1], (LAYERS, D, R), D ** -0.5, 0.1875, ((0, 4),), jnp.float32),
        "inputs": gaussian(key_list[2], (LAYERS, TOKENS, D), 1.0, 6.0, ((0, 4), (1, 2))),
        "out_grads": gaussian(key_list[3], (LAYERS, TOKENS, F), TOKENS ** -0.5, 0.25, ((0, 4), (1, 2), (2, 4))),
        "first_moment": gaussian(key_list[4], (LAYERS, R, F), 1.0, 6.0, ((0, 4), (1, 2), (2, 4)), jnp.float32),
        "second_moment": jnp.clip(jnp.exp(math.log(1.0) - 4.6051702 * jax.random.uniform(key_list[5], (LAYERS, R, F), jnp.float32) ** steps_of(key_list[5], (LAYERS, R, F), ((0, 4), (1, 2), (2, 4)), -0.2, 0.2)), 0.01, 1.0),
    }


beta_one = 0.9
beta_two = 0.99
bias_one = 1.0 - 0.9 ** 10
bias_two = 1.0 - 0.99 ** 10
adam_eps = 1e-08
norm_eps = 1e-06
step_rate = 0.2
quintic_one = 3.4445
quintic_two = -4.775
quintic_three = 2.0315

def quintic(matrix):
    for sweep in range(ITERS):
        gram = jnp.dot(matrix.T, matrix, precision=lax.Precision.HIGHEST)
        poly = quintic_two * gram + quintic_three * jnp.dot(gram, gram, precision=lax.Precision.HIGHEST)
        matrix = quintic_one * matrix + jnp.dot(matrix, poly, precision=lax.Precision.HIGHEST)
    return matrix

def one_layer(weight, basis, inputs, out_grads, first_moment, second_moment):
    gradient = jnp.dot(inputs.T, out_grads, preferred_element_type=jnp.float32)
    coeffs = jnp.dot(basis.T, gradient, precision=lax.Precision.HIGHEST)
    first = beta_one * first_moment + (1.0 - beta_one) * coeffs
    second = beta_two * second_moment + (1.0 - beta_two) * coeffs * coeffs
    direction = first / bias_one / (jnp.sqrt(second / bias_two) + adam_eps)
    updated = weight - step_rate * jnp.dot(basis, direction, precision=lax.Precision.HIGHEST)
    subspace = jnp.dot(gradient, coeffs.T, precision=lax.Precision.HIGHEST)
    start_point = subspace / jnp.sqrt(jnp.sum(subspace * subspace) + norm_eps)
    return (updated, quintic(start_point), first, second)

def reference(weight, basis, inputs, out_grads, first_moment, second_moment):
    results = [one_layer(weight[which], basis[which], inputs[which], out_grads[which], first_moment[which], second_moment[which]) for which in range(LAYERS)]
    return (jnp.stack([item[0] for item in results]), jnp.stack([item[1] for item in results]), jnp.stack([item[2] for item in results]), jnp.stack([item[3] for item in results]))
```

```python
import jax
import jax.numpy as jnp
from jax import lax
from jax.sharding import PartitionSpec as P

ITERS = 5


beta_one = 0.9
beta_two = 0.99
bias_one = 1.0 - 0.9**10
bias_two = 1.0 - 0.99**10
adam_eps = 1e-08
norm_eps = 1e-06
step_rate = 0.2
quintic_one = 3.4445
quintic_two = -4.775
quintic_three = 2.0315

HI = lax.Precision.HIGHEST


def quintic(matrix):
    for sweep in range(ITERS):
        gram = jnp.dot(matrix.T, matrix, precision=HI)
        poly = quintic_two * gram + quintic_three * jnp.dot(gram, gram, precision=HI)
        matrix = quintic_one * matrix + jnp.dot(matrix, poly, precision=HI)
    return matrix


def adam(coef_own, first_moment, second_moment):
    first = beta_one * first_moment + (1.0 - beta_one) * coef_own
    second = beta_two * second_moment + (1.0 - beta_two) * coef_own * coef_own
    direct_own = first / bias_one / (jnp.sqrt(second / bias_two) + adam_eps)
    return first, second, direct_own


def general(weight, basis, inputs, out_grads, first_moment, second_moment):
    shard_idx = lax.axis_index("shards")
    basis_now = basis[0]
    gradient = lax.psum(
        jnp.dot(inputs[0].T, out_grads[0], preferred_element_type=jnp.float32), "shards"
    )
    coeffs = jnp.dot(basis_now.T, gradient, precision=HI)
    rank_rows = first_moment.shape[1]
    coef_own = lax.dynamic_slice_in_dim(coeffs, shard_idx * rank_rows, rank_rows, 0)
    first, second, direct_own = adam(coef_own, first_moment[0], second_moment[0])
    direction = lax.all_gather(direct_own, "shards", axis=0, tiled=True)
    updated = weight[0] - step_rate * jnp.dot(basis_now, direction, precision=HI)
    subspace = lax.psum(jnp.dot(gradient, coeffs.T, precision=HI), "tensor")
    start_point = subspace / jnp.sqrt(jnp.sum(subspace * subspace) + norm_eps)
    return updated[None], quintic(start_point)[None], first[None], second[None]


def nn(a, b):
    return jnp.dot(a, b, precision=HI, preferred_element_type=jnp.float32)


def nt(a, b):
    return lax.dot_general(
        a, b, (((1,), (1,)), ((), ())), precision=HI, preferred_element_type=jnp.float32
    )


def gram_quintic(gram):
    total = None
    for sweep in range(ITERS):
        poly = quintic_two * gram + quintic_three * nn(gram, gram)
        if total is None:
            total = quintic_one * jnp.eye(gram.shape[0], dtype=jnp.float32) + poly
        else:
            total = quintic_one * total + nn(total, poly)
        if sweep < ITERS - 1:
            half = quintic_one * gram + nn(gram, poly)
            gram = quintic_one * half + nn(half, poly)
    return total


def paired(weight, basis, inputs, out_grads, first_moment, second_moment):
    shard_idx = lax.axis_index("shards")
    swap = lambda a: lax.ppermute(a, "shards", [(0, 1), (1, 0)])
    send = lambda a, m: lax.ppermute(a, "tensor", [(t, t ^ m) for t in range(4)])
    basis_now = basis[0]
    x_own = inputs[0].astype(jnp.float32)
    y_own = out_grads[0].astype(jnp.float32)
    ys = [y_own] + [send(y_own, m) for m in (1, 2, 3)]
    x_oth = swap(x_own)
    yo = [swap(y) for y in ys]
    basis_t = basis_now.T
    p_own, p_oth = nt(basis_t, x_own), nt(basis_t, x_oth)
    kern = [[nt(x_own, x_own), nt(x_own, x_oth)], [nt(x_oth, x_own), nt(x_oth, x_oth)]]
    cs = [nn(p_own, a) + nn(p_oth, b) for a, b in zip(ys, yo)]
    rank_rows = first_moment.shape[1]
    coef_own = lax.dynamic_slice_in_dim(cs[0], shard_idx * rank_rows, rank_rows, 0)
    first, second, direct_own = adam(coef_own, first_moment[0], second_moment[0])
    direct_oth = swap(direct_own)
    halves = [
        lax.dynamic_slice_in_dim(basis_now, s * rank_rows, rank_rows, 1)
        for s in (shard_idx, 1 - shard_idx)
    ]
    updated = weight[0] - step_rate * (nn(halves[0], direct_own) + nn(halves[1], direct_oth))
    four = lambda t: (t[0] + t[1]) + (t[2] + t[3])
    z_own = four([nt(c, y) for c, y in zip(cs, ys)])
    z_oth = four([nt(c, y) for c, y in zip(cs, yo)])
    zk = [nn(z_own, kern[0][j]) + nn(z_oth, kern[1][j]) for j in range(2)]
    gram = nt(zk[0], z_own) + nt(zk[1], z_oth)
    inverse = 1.0 / (jnp.trace(gram) + norm_eps)
    total = gram_quintic(gram * inverse) * jnp.sqrt(inverse)
    refreshed = nt(x_own.T, nn(total, z_own)) + nt(x_oth.T, nn(total, z_oth))
    return updated[None], refreshed[None], first[None], second[None]


def solution(mesh):
    placed = (
        P("sections", None, "tensor"),
        P("sections", None, None),
        P("sections", "shards", None),
        P("sections", "shards", "tensor"),
        P("sections", "shards", "tensor"),
        P("sections", "shards", "tensor"),
    )
    fits = mesh.shape["shards"] == 2 and mesh.shape["tensor"] == 4
    return jax.shard_map(
        paired if fits else general,
        mesh=mesh,
        in_specs=placed,
        out_specs=(
            P("sections", None, "tensor"),
            P("sections", None, None),
            P("sections", "shards", "tensor"),
            P("sections", "shards", "tensor"),
        ),
        check_vma=False,
    )
```

```python
import jax
import jax.numpy as jnp
from jax import lax
from jax.experimental import pallas as pl
from jax.experimental.pallas import tpu as pltpu
from jax.sharding import PartitionSpec as P

ITERS = 5


beta_one = 0.9
beta_two = 0.99
bias_one = 1.0 - 0.9**10
bias_two = 1.0 - 0.99**10
adam_eps = 1e-08
norm_eps = 1e-06
step_rate = 0.2
quintic_one = 3.4445
quintic_two = -4.775
quintic_three = 2.0315

HI = lax.Precision.HIGHEST


def quintic(matrix):
    for sweep in range(ITERS):
        gram = jnp.dot(matrix.T, matrix, precision=HI)
        poly = quintic_two * gram + quintic_three * jnp.dot(gram, gram, precision=HI)
        matrix = quintic_one * matrix + jnp.dot(matrix, poly, precision=HI)
    return matrix


def adam(coef_own, first_moment, second_moment):
    first = beta_one * first_moment + (1.0 - beta_one) * coef_own
    second = beta_two * second_moment + (1.0 - beta_two) * coef_own * coef_own
    direct_own = first / bias_one / (jnp.sqrt(second / bias_two) + adam_eps)
    return first, second, direct_own


def general(weight, basis, inputs, out_grads, first_moment, second_moment):
    shard_idx = lax.axis_index("shards")
    basis_now = basis[0]
    gradient = lax.psum(
        jnp.dot(inputs[0].T, out_grads[0], preferred_element_type=jnp.float32), "shards"
    )
    coeffs = jnp.dot(basis_now.T, gradient, precision=HI)
    rank_rows = first_moment.shape[1]
    coef_own = lax.dynamic_slice_in_dim(coeffs, shard_idx * rank_rows, rank_rows, 0)
    first, second, direct_own = adam(coef_own, first_moment[0], second_moment[0])
    direction = lax.all_gather(direct_own, "shards", axis=0, tiled=True)
    updated = weight[0] - step_rate * jnp.dot(basis_now, direction, precision=HI)
    subspace = lax.psum(jnp.dot(gradient, coeffs.T, precision=HI), "tensor")
    start_point = subspace / jnp.sqrt(jnp.sum(subspace * subspace) + norm_eps)
    return updated[None], quintic(start_point)[None], first[None], second[None]


F32, BF16 = jnp.float32, jnp.bfloat16
VMEM = pltpu.VMEM


def nn(a, b):
    return lax.dot_general(a, b, (((1,), (0,)), ((), ())), preferred_element_type=F32)


def nt(a, b):
    return lax.dot_general(a, b, (((1,), (1,)), ((), ())), preferred_element_type=F32)


def parts(x, n):
    out = []
    for i in range(n):
        out.append(x.astype(BF16))
        if i < n - 1:
            x = x - out[-1].astype(F32)
    return out


def left(dot, pieces, b):
    terms = [dot(p, b) for p in reversed(pieces)]
    return sum(terms[1:], terms[0])


def both(dot, a, b):
    return (dot(a[0], b[1]) + dot(a[1], b[0])) + dot(a[0], b[0])


def cast_kernel(a_ref, o_ref):
    o_ref[...] = a_ref[...].astype(o_ref.dtype)


def project(x, basis_ref, pt_ref, step=256):
    total = None
    for k in range(0, basis_ref.shape[0], step):
        for piece in reversed(parts(basis_ref[pl.ds(k, step), :], 3)):
            term = nn(x[:, k : k + step], piece)
            total = term if total is None else total + term
    for i, piece in enumerate(parts(total.T, 3)):
        pt_ref[i] = piece


def join_kernel(x_ref, y_ref, o_ref):
    width = x_ref.shape[1]
    o_ref[:, :width] = x_ref[...].astype(F32)
    o_ref[:, width:] = y_ref[...]


def own_kernel(xy_ref, basis_ref, pt_ref, k_ref, xt_ref):
    x32 = xy_ref[:, : basis_ref.shape[0]]
    x = x32.astype(BF16)
    project(x, basis_ref, pt_ref)
    for i, piece in enumerate(parts(nt(x, x), 2)):
        k_ref[i] = piece
    xt_ref[...] = x32.T.astype(BF16)


def other_kernel(xy_ref, xyo_ref, basis_ref, pt_ref, kxo_ref, kox_ref, kxx_ref, xt_ref):
    width = basis_ref.shape[0]
    x32 = xy_ref[:, :width]
    x = x32.astype(BF16)
    xo = xyo_ref[:, :width].astype(BF16)
    project(x, basis_ref, pt_ref)
    for a, b, ref in ((x, xo, kxo_ref), (xo, x, kox_ref), (x, x, kxx_ref)):
        for i, piece in enumerate(parts(nt(a, b), 2)):
            ref[i] = piece
    xt_ref[...] = x32.T.astype(BF16)


def coefficients(pto_ref, ptx_ref, yo, yx):
    own = left(nn, [pto_ref[i] for i in range(3)], yo)
    return own + left(nn, [ptx_ref[i] for i in range(3)], yx)


def moment_kernel(idx_ref, pto_ref, ptx_ref, yo_ref, xyx_ref, m_ref, v_ref,
                  first_ref, second_ref, dir_ref, zo_ref, zx_ref, c_ref):
    yo = yo_ref[...].astype(BF16)
    yx = xyx_ref[:, xyx_ref.shape[1] - yo.shape[1] :].astype(BF16)
    c = coefficients(pto_ref, ptx_ref, yo, yx)
    c_ref[...] = c
    rows = m_ref.shape[0]
    own = c_ref[pl.ds(pl.multiple_of(idx_ref[0] * rows, rows), rows), :]
    first = beta_one * m_ref[...] + (1.0 - beta_one) * own
    second = beta_two * v_ref[...] + (1.0 - beta_two) * own * own
    first_ref[...] = first
    second_ref[...] = second
    dir_ref[...] = first / bias_one / (jnp.sqrt(second / bias_two) + adam_eps)
    pieces = parts(c, 3)
    zo_ref[...] = left(nt, pieces, yo)
    zx_ref[...] = left(nt, pieces, yx)


def block_kernel(pto_ref, ptx_ref, yo_ref, yx_ref, zo_ref, zx_ref):
    yo, yx = yo_ref[...].astype(BF16), yx_ref[...].astype(BF16)
    pieces = parts(coefficients(pto_ref, ptx_ref, yo, yx), 3)
    zo_ref[...] = left(nt, pieces, yo)
    zx_ref[...] = left(nt, pieces, yx)


def weight_kernel(idx_ref, w_ref, basis_ref, do_ref, dx_ref, o_ref, dir_ref):
    rows = do_ref.shape[0]

    @pl.when(pl.program_id(0) == 0)
    def _():
        for which, ref in ((idx_ref[0], do_ref), (1 - idx_ref[0], dx_ref)):
            for i, piece in enumerate(parts(ref[...], 2)):
                dir_ref[i, pl.ds(pl.multiple_of(which * rows, rows), rows), :] = piece

    direction = [dir_ref[0], dir_ref[1]]
    o_ref[...] = w_ref[...] - step_rate * both(nn, parts(basis_ref[...], 2), direction)


def gram_quintic(gram):
    total = None
    for sweep in range(ITERS):
        g = parts(gram, 2)
        poly = quintic_two * gram + quintic_three * both(nn, g, g)
        p = parts(poly, 2)
        if total is None:
            r = lax.broadcasted_iota(jnp.int32, gram.shape, 0)
            c = lax.broadcasted_iota(jnp.int32, gram.shape, 1)
            total = jnp.where(r == c, quintic_one + poly, poly)
        else:
            total = quintic_one * total + both(nn, parts(total, 2), p)
        if sweep < ITERS - 1:
            half = quintic_one * gram + both(nn, g, p)
            gram = quintic_one * half + both(nn, parts(half, 2), p)
    return total


def basis_kernel(pto_ref, ptx_ref, yo_ref, yx_ref, z1o, z1x, z2o, z2x, z3o, z3x,
                 koo, kox, kxo, kxx, xto_ref, xtx_ref, o_ref, buf, sems):
    yo, yx = yo_ref[...].astype(BF16), yx_ref[...].astype(BF16)
    pieces = parts(coefficients(pto_ref, ptx_ref, yo, yx), 3)
    zo = (z1o[...] + z2o[...]) + (z3o[...] + left(nt, pieces, yo))
    zx = (z1x[...] + z2x[...]) + (z3x[...] + left(nt, pieces, yx))
    zo2, zx2 = parts(zo, 2), parts(zx, 2)
    two = lambda ref: [ref[0], ref[1]]
    zko = both(nn, zo2, two(koo)) + both(nn, zx2, two(kxo))
    zkx = both(nn, zo2, two(kox)) + both(nn, zx2, two(kxx))
    gram = both(nt, parts(zko, 2), zo2) + both(nt, parts(zkx, 2), zx2)
    r = lax.broadcasted_iota(jnp.int32, gram.shape, 0)
    c = lax.broadcasted_iota(jnp.int32, gram.shape, 1)
    trace = jnp.sum(jnp.where(r == c, gram, 0.0), keepdims=True)
    inverse = 1.0 / (trace + norm_eps)
    total = parts(gram_quintic(gram * inverse) * jnp.sqrt(inverse), 2)
    wo = parts(both(nn, total, zo2), 2)
    wx = parts(both(nn, total, zx2), 2)
    n = sems.shape[0]
    rows = o_ref.shape[0] // n
    copies = []
    for i in range(n):
        at = pl.ds(i * rows, rows)
        xo, xx = xto_ref[at, :], xtx_ref[at, :]
        buf[at, :] = (nt(xo, wo[1]) + nt(xo, wo[0])) + (nt(xx, wx[1]) + nt(xx, wx[0]))
        copies.append(pltpu.make_async_copy(buf.at[at, :], o_ref.at[at, :], sems.at[i]))
        copies[-1].start()
    for copy in copies:
        copy.wait()


def call(kernel, outs, ins, scratch=(), cost=0, name=None, **more):
    return pl.pallas_call(
        kernel,
        out_shape=outs,
        scratch_shapes=scratch,
        name=name,
        cost_estimate=pl.CostEstimate(flops=cost, bytes_accessed=4 << 20, transcendentals=0),
        compiler_params=pltpu.CompilerParams(vmem_limit_bytes=20 << 20),
        **more,
    )(*ins)


def paired(weight, basis, inputs, out_grads, first_moment, second_moment):
    tokens, width = inputs.shape[1:]
    features, rank = out_grads.shape[2], basis.shape[2]
    rows = first_moment.shape[1]
    idx = lax.axis_index("shards").astype(jnp.int32).reshape(1)
    swap = lambda a: lax.ppermute(a, "shards", [(0, 1), (1, 0)])

    def send(a, masks):
        pairs = [(s * 4 + t, s * 4 + (t ^ masks[s])) for s in range(2) for t in range(4)]
        return lax.ppermute(a, ("shards", "tensor"), pairs)

    sds = jax.ShapeDtypeStruct
    vm = pl.BlockSpec(memory_space=VMEM)
    sm = pl.BlockSpec(memory_space=pltpu.SMEM)
    def run(kernel, outs, ins, cost, scratch=(), in_specs=None, out_specs=None, name=None):
        return call(kernel, outs, ins, scratch, cost, name,
                    in_specs=in_specs or [vm] * len(ins),
                    out_specs=out_specs or jax.tree.map(lambda _: vm, outs))

    after = lax.optimization_barrier
    basis_now, x_bf, y_bf = basis[0], inputs[0], out_grads[0]
    idx, y_bf = after((idx, y_bf))
    y_own = run(cast_kernel, VMEM(y_bf.shape, F32), [y_bf], 10, name="cast_y")
    y_one, y_two = send(y_own, (1, 2)), send(y_own, (2, 1))
    xy = run(join_kernel, VMEM((tokens, width + features), F32), [x_bf, y_own], 10, name="join")
    xy_oth = swap(xy)
    split3 = VMEM((3, rank, tokens), BF16)
    split2 = VMEM((2, tokens, tokens), BF16)
    turned = VMEM((width, tokens), BF16)
    pto, koo, xto = run(own_kernel, (split3, split2, turned), [xy, basis_now], 100, name="own")
    xy_oth, pto = after((xy_oth, pto))
    ptx, kxo, kox, kxx, xtx = run(
        other_kernel, (split3, split2, split2, split2, turned), [xy_oth, xy, basis_now], 100, name="other"
    )
    y_one, ptx = after((y_one, ptx))
    y_three = send(y_one, (2, 1))
    y_one_oth = swap(y_one)
    zt = VMEM((rank, tokens), F32)
    small = sds((rows, features), F32)
    first, second, d_own, z1o, z1x = run(
        moment_kernel, (small, small, small, zt, zt),
        [idx, pto, ptx, y_own, xy_oth, first_moment[0], second_moment[0]], 100,
        scratch=[VMEM((rank, features), F32)], in_specs=[sm] + [vm] * 6, name="moments",
    )
    d_oth = swap(d_own)
    y_two, d_own = after((y_two, d_own))
    y_two_oth = swap(y_two)
    n = 4
    block = pl.BlockSpec((width // n, features), lambda i: (i, 0))
    whole = pl.BlockSpec((rows, features), lambda i: (0, 0))
    updated = call(
        weight_kernel, sds(weight.shape[1:], F32), [idx, weight[0], basis_now, d_own, d_oth],
        [VMEM((2, rank, features), BF16)], 100, "weights",
        grid=(n,),
        in_specs=[sm, block, pl.BlockSpec((width // n, rank), lambda i: (i, 0)), whole, whole],
        out_specs=block,
    )
    y_three, updated, ptx = after((y_three, updated, ptx))
    y_three_oth = swap(y_three)
    z2o, z2x = run(block_kernel, (zt, zt), [pto, ptx, y_one, y_two_oth], 100, name="block1")
    z3o, z3x = run(block_kernel, (zt, zt), [pto, ptx, y_two, y_one_oth], 100, name="block2")
    y_three_oth, z2o, z3o = after((y_three_oth, z2o, z3o))
    refreshed = run(
        basis_kernel, sds((width, rank), F32),
        [pto, ptx, y_three, y_three_oth, z1o, z1x, z2o, z2x, z3o, z3x, koo, kox, kxo, kxx, xto, xtx], 100,
        scratch=[VMEM((width, rank), F32), pltpu.SemaphoreType.DMA((4,))],
        out_specs=pl.BlockSpec(memory_space=pl.ANY), name="basis",
    )
    return updated[None], refreshed[None], first[None], second[None]


def solution(mesh):
    placed = (
        P("sections", None, "tensor"),
        P("sections", None, None),
        P("sections", "shards", None),
        P("sections", "shards", "tensor"),
        P("sections", "shards", "tensor"),
        P("sections", "shards", "tensor"),
    )
    fits = mesh.shape["shards"] == 2 and mesh.shape["tensor"] == 4
    return jax.shard_map(
        paired if fits else general,
        mesh=mesh,
        in_specs=placed,
        out_specs=(
            P("sections", None, "tensor"),
            P("sections", None, None),
            P("sections", "shards", "tensor"),
            P("sections", "shards", "tensor"),
        ),
        check_vma=False,
    )
```

```python
import jax
import jax.numpy as jnp
from jax import lax
from jax.experimental import pallas as pl
from jax.experimental.pallas import tpu as pltpu
from jax.sharding import PartitionSpec as P

ITERS = 5


beta_one = 0.9
beta_two = 0.99
bias_one = 1.0 - 0.9**10
bias_two = 1.0 - 0.99**10
adam_eps = 1e-08
norm_eps = 1e-06
step_rate = 0.2
quintic_one = 3.4445
quintic_two = -4.775
quintic_three = 2.0315

HI = lax.Precision.HIGHEST


def quintic(matrix):
    for sweep in range(ITERS):
        gram = jnp.dot(matrix.T, matrix, precision=HI)
        poly = quintic_two * gram + quintic_three * jnp.dot(gram, gram, precision=HI)
        matrix = quintic_one * matrix + jnp.dot(matrix, poly, precision=HI)
    return matrix


def adam(coef_own, first_moment, second_moment):
    first = beta_one * first_moment + (1.0 - beta_one) * coef_own
    second = beta_two * second_moment + (1.0 - beta_two) * coef_own * coef_own
    direct_own = first / bias_one / (jnp.sqrt(second / bias_two) + adam_eps)
    return first, second, direct_own


def general(weight, basis, inputs, out_grads, first_moment, second_moment):
    shard_idx = lax.axis_index("shards")
    basis_now = basis[0]
    gradient = lax.psum(
        jnp.dot(inputs[0].T, out_grads[0], preferred_element_type=jnp.float32), "shards"
    )
    coeffs = jnp.dot(basis_now.T, gradient, precision=HI)
    rank_rows = first_moment.shape[1]
    coef_own = lax.dynamic_slice_in_dim(coeffs, shard_idx * rank_rows, rank_rows, 0)
    first, second, direct_own = adam(coef_own, first_moment[0], second_moment[0])
    direction = lax.all_gather(direct_own, "shards", axis=0, tiled=True)
    updated = weight[0] - step_rate * jnp.dot(basis_now, direction, precision=HI)
    subspace = lax.psum(jnp.dot(gradient, coeffs.T, precision=HI), "tensor")
    start_point = subspace / jnp.sqrt(jnp.sum(subspace * subspace) + norm_eps)
    return updated[None], quintic(start_point)[None], first[None], second[None]


F32, BF16 = jnp.float32, jnp.bfloat16
VMEM = pltpu.VMEM
PARTS = 2


def nn(a, b):
    return lax.dot_general(a, b, (((1,), (0,)), ((), ())), preferred_element_type=F32)


def nt(a, b):
    return lax.dot_general(a, b, (((1,), (1,)), ((), ())), preferred_element_type=F32)


def parts(x, n):
    out = []
    for i in range(n):
        out.append(x.astype(BF16))
        if i < n - 1:
            x = x - out[-1].astype(F32)
    return out


def left(dot, pieces, b):
    terms = [dot(p, b) for p in reversed(pieces)]
    return sum(terms[1:], terms[0])


def both(dot, a, b):
    return (dot(a[0], b[1]) + dot(a[1], b[0])) + dot(a[0], b[0])


def first_kernel(x_hbm, y_hbm, basis_hbm, c_ref, x_ref, y_ref, basis_ref, sems):
    n = sems.shape[0] - 2
    rows = basis_ref.shape[0] // n
    spans = [pl.ds(i * rows, rows) for i in range(n)]
    x_copy = pltpu.make_async_copy(x_hbm, x_ref, sems.at[n])
    y_copy = pltpu.make_async_copy(y_hbm, y_ref, sems.at[n + 1])
    copies = [
        pltpu.make_async_copy(basis_hbm.at[at, :], basis_ref.at[at, :], sems.at[i])
        for i, at in enumerate(spans)
    ]
    for copy in (x_copy, *copies, y_copy):
        copy.start()
    x_copy.wait()
    total = None
    for copy, at in zip(copies, spans):
        copy.wait()
        hi, lo = parts(basis_ref[at, :], 2)
        x = x_ref[:, at]
        term = nn(x, lo) + nn(x, hi)
        total = term if total is None else total + term
    y_copy.wait()
    c_ref[...] = left(nn, parts(total.T, PARTS), y_ref[...])


def own_kernel(x_ref, x32_ref, k_ref, xt_ref):
    x = x_ref[...]
    x32 = x.astype(F32)
    x32_ref[...] = x32
    for i, piece in enumerate(parts(nt(x, x), PARTS)):
        k_ref[i] = piece
    xt_ref[...] = x32.T.astype(BF16)


def other_kernel(x_ref, xo_ref, kox_ref, kxx_ref, xt_ref):
    x32 = x_ref[...]
    x = x32.astype(BF16)
    for a, ref in ((xo_ref[...], kox_ref), (x, kxx_ref)):
        for i, piece in enumerate(parts(nt(a, x), PARTS)):
            ref[i] = piece
    xt_ref[...] = x32.T.astype(BF16)


def moment_kernel(co_ref, cx_ref, y_ref, m_ref, v_ref, first_ref, second_ref, dir_ref, z_ref, c_ref):
    c = co_ref[...] + cx_ref[...]
    c_ref[...] = c
    z_ref[...] = left(nt, parts(c, PARTS), y_ref[...])
    rows = m_ref.shape[0]
    own = c_ref[pl.ds(pl.multiple_of(lax.axis_index("shards") * rows, rows), rows), :]
    first = beta_one * m_ref[...] + (1.0 - beta_one) * own
    second = beta_two * v_ref[...] + (1.0 - beta_two) * own * own
    first_ref[...] = first
    second_ref[...] = second
    dir_ref[...] = first / bias_one / (jnp.sqrt(second / bias_two) + adam_eps)


def add_kernel(a_ref, b_ref, o_ref):
    o_ref[...] = a_ref[...] + b_ref[...]


def weight_kernel(w_ref, basis_ref, do_ref, dx_ref, m_ref, v_ref,
                  o_ref, first_ref, second_ref, dir_ref, buf, sems):
    rows = do_ref.shape[0]
    copies = [
        pltpu.make_async_copy(m_ref, first_ref, sems.at[0]),
        pltpu.make_async_copy(v_ref, second_ref, sems.at[1]),
    ]
    for copy in copies:
        copy.start()
    shard = lax.axis_index("shards")
    for which, ref in ((shard, do_ref), (1 - shard, dx_ref)):
        for i, piece in enumerate(parts(ref[...], 2)):
            dir_ref[i, pl.ds(pl.multiple_of(which * rows, rows), rows), :] = piece
    direction = [dir_ref[0], dir_ref[1]]
    n = sems.shape[0] - 2
    rows = o_ref.shape[0] // n
    for i in range(n):
        at = pl.ds(i * rows, rows)
        step = both(nn, parts(basis_ref[at, :], 2), direction)
        buf[at, :] = w_ref[at, :] - step_rate * step
        copies.append(pltpu.make_async_copy(buf.at[at, :], o_ref.at[at, :], sems.at[2 + i]))
        copies[-1].start()
    for copy in copies:
        copy.wait()


def stacked(a, b):
    n = a[0].shape[0]
    terms = nn(jnp.concatenate(a, 0), b[0])
    return (terms[n:] + nn(a[0], b[1])) + terms[:n]


def gram_quintic(gram):
    n = gram.shape[0] // 2
    whole = lambda halves: [jnp.concatenate(h, 0) for h in zip(*halves)]
    rows = [gram[:n], gram[n:]]
    total = None
    for sweep in range(ITERS):
        g = [parts(h, 2) for h in rows]
        square = whole(g)
        poly = [quintic_two * h + quintic_three * stacked(p, square) for h, p in zip(rows, g)]
        p = whole([parts(h, 2) for h in poly])
        if total is None:
            r = lax.broadcasted_iota(jnp.int32, gram.shape, 0)
            c = lax.broadcasted_iota(jnp.int32, gram.shape, 1)
            first = jnp.where(r == c, quintic_one, 0.0)
            total = [first[:n] + poly[0], first[n:] + poly[1]]
        else:
            total = [quintic_one * t + stacked(parts(t, 2), p) for t in total]
        if sweep < ITERS - 1:
            half = [quintic_one * h + stacked(q, p) for h, q in zip(rows, g)]
            rows = [quintic_one * h + stacked(parts(h, 2), p) for h in half]
    return jnp.concatenate(total, 0)


def early_kernel(zo_ref, koo_ref, kox_ref, gram_ref, mixed_ref, zo2_ref):
    zo2 = parts(zo_ref[...], 2)
    gram_ref[...] = both(nt, parts(both(nn, zo2, [koo_ref[0], koo_ref[1]]), 2), zo2)
    mixed = parts(both(nn, zo2, [kox_ref[0], kox_ref[1]]), 2)
    for i in range(2):
        mixed_ref[i] = mixed[i]
        zo2_ref[i] = zo2[i]


def basis_kernel(gram_ref, mixed_ref, zo2_ref, zx_ref, kxx_ref, xto_ref, xtx_ref, o_ref, buf, sems):
    zo2, zx2 = [zo2_ref[0], zo2_ref[1]], parts(zx_ref[...], 2)
    cross = both(nt, [mixed_ref[0], mixed_ref[1]], zx2)
    gram = both(nt, parts(both(nn, zx2, [kxx_ref[0], kxx_ref[1]]), 2), zx2)
    gram = (gram_ref[...] + gram) + (cross + cross.T)
    r = lax.broadcasted_iota(jnp.int32, gram.shape, 0)
    c = lax.broadcasted_iota(jnp.int32, gram.shape, 1)
    trace = jnp.sum(jnp.where(r == c, gram, 0.0), keepdims=True)
    inverse = 1.0 / (trace + norm_eps)
    total = parts(gram_quintic(gram * inverse) * jnp.sqrt(inverse), 2)
    wo = parts(both(nn, total, zo2), 2)
    wx = parts(both(nn, total, zx2), 2)
    n = sems.shape[0]
    rows = o_ref.shape[0] // n
    copies = []
    for i in range(n):
        at = pl.ds(i * rows, rows)
        xo, xx = xto_ref[at, :], xtx_ref[at, :]
        buf[at, :] = (nt(xo, wo[1]) + nt(xo, wo[0])) + (nt(xx, wx[1]) + nt(xx, wx[0]))
        copies.append(pltpu.make_async_copy(buf.at[at, :], o_ref.at[at, :], sems.at[i]))
        copies[-1].start()
    for copy in copies:
        copy.wait()


def call(kernel, outs, ins, scratch=(), cost=0, name=None, **more):
    return pl.pallas_call(
        kernel,
        out_shape=outs,
        scratch_shapes=scratch,
        name=name,
        cost_estimate=pl.CostEstimate(flops=cost, bytes_accessed=4 << 20, transcendentals=0),
        compiler_params=pltpu.CompilerParams(vmem_limit_bytes=20 << 20),
        **more,
    )(*ins)


def paired(weight, basis, inputs, out_grads, first_moment, second_moment):
    tokens, width = inputs.shape[1:]
    features, rank = out_grads.shape[2], basis.shape[2]
    rows = first_moment.shape[1]
    swap = lambda a: lax.ppermute(a, "shards", [(0, 1), (1, 0)])

    def send(a, masks):
        pairs = [(s * 4 + t, s * 4 + (t ^ masks[s])) for s in range(2) for t in range(4)]
        return lax.ppermute(a, ("shards", "tensor"), pairs)

    sds = jax.ShapeDtypeStruct
    vm = pl.BlockSpec(memory_space=VMEM)
    def run(kernel, outs, ins, cost, scratch=(), in_specs=None, out_specs=None, name=None):
        return call(kernel, outs, ins, scratch, cost, name,
                    in_specs=in_specs or [vm] * len(ins),
                    out_specs=out_specs or jax.tree.map(lambda _: vm, outs))

    after = lax.optimization_barrier
    far = pl.BlockSpec(memory_space=pl.ANY)
    hbm = [pltpu.with_memory_space_constraint(a[0], pltpu.HBM) for a in (inputs, out_grads, basis)]
    square = (rank, features)
    c_own, x_bf, y_own, basis_now = run(
        first_kernel,
        (VMEM(square, F32), VMEM((tokens, width), BF16), VMEM((tokens, features), BF16), VMEM((width, rank), F32)),
        hbm, 100,
        scratch=[pltpu.SemaphoreType.DMA((3,))],
        in_specs=[pl.BlockSpec(memory_space=pltpu.HBM)] * 3, name="coefficients",
    )
    c_oth = swap(c_own)
    kept = VMEM((PARTS, tokens, tokens), BF16)
    turned = VMEM((width, tokens), BF16)
    x_own, koo, xto = run(own_kernel, (VMEM((tokens, width), F32), kept, turned), [x_bf], 100, name="own")
    x_own, koo, c_oth = after((x_own, koo, c_oth))
    x_oth = swap(x_own)
    zt = VMEM((rank, tokens), F32)
    small = VMEM((rows, features), F32)
    first, second, d_own, z_one = run(
        moment_kernel, (small, small, small, zt),
        [c_own, c_oth, y_own, first_moment[0], second_moment[0]], 100,
        scratch=[VMEM(square, F32)], name="moments",
    )
    z_got = send(z_one, (1, 2))
    x_oth, d_own = after((x_oth, d_own))
    kox, kxx, xtx = run(
        other_kernel, (kept, kept, turned), [x_oth, x_bf], 100, name="other"
    )
    z_got, kxx = after((z_got, kxx))
    z_two = run(add_kernel, zt, [z_one, z_got], 100, name="add1")
    z_got = send(z_two, (2, 1))
    d_own, z_two = after((d_own, z_two))
    d_oth = swap(d_own)
    updated, first, second = run(
        weight_kernel, (sds(weight.shape[1:], F32), sds(first.shape, F32), sds(second.shape, F32)),
        [weight[0], basis_now, d_own, d_oth, first, second], 100,
        scratch=[VMEM((2, rank, features), BF16), VMEM((width, features), F32), pltpu.SemaphoreType.DMA((6,))],
        out_specs=(far, far, far), name="weights",
    )
    z_got, updated = after((z_got, updated))
    z_own = run(add_kernel, zt, [z_two, z_got], 100, name="add2")
    z_oth = swap(z_own)
    gram, mixed, zo2 = run(
        early_kernel, (VMEM((rank, rank), F32), VMEM((2, rank, tokens), BF16), VMEM((2, rank, tokens), BF16)),
        [z_own, koo, kox], 100, name="early",
    )
    z_oth, gram = after((z_oth, gram))
    refreshed = run(
        basis_kernel, sds((width, rank), F32),
        [gram, mixed, zo2, z_oth, kxx, xto, xtx], 100,
        scratch=[VMEM((width, rank), F32), pltpu.SemaphoreType.DMA((4,))],
        out_specs=far, name="basis",
    )
    return updated[None], refreshed[None], first[None], second[None]


def solution(mesh):
    placed = (
        P("sections", None, "tensor"),
        P("sections", None, None),
        P("sections", "shards", None),
        P("sections", "shards", "tensor"),
        P("sections", "shards", "tensor"),
        P("sections", "shards", "tensor"),
    )
    fits = mesh.shape["shards"] == 2 and mesh.shape["tensor"] == 4
    return jax.shard_map(
        paired if fits else general,
        mesh=mesh,
        in_specs=placed,
        out_specs=(
            P("sections", None, "tensor"),
            P("sections", None, None),
            P("sections", "shards", "tensor"),
            P("sections", "shards", "tensor"),
        ),
        check_vma=False,
    )
```

```python
import jax
import jax.numpy as jnp
from jax import lax
from jax.experimental import pallas as pl
from jax.experimental.pallas import tpu as pltpu
from jax.sharding import PartitionSpec as P

ITERS = 5


beta_one = 0.9
beta_two = 0.99
bias_one = 1.0 - 0.9**10
bias_two = 1.0 - 0.99**10
adam_eps = 1e-08
norm_eps = 1e-06
step_rate = 0.2
quintic_one = 3.4445
quintic_two = -4.775
quintic_three = 2.0315

HI = lax.Precision.HIGHEST


def quintic(matrix):
    for sweep in range(ITERS):
        gram = jnp.dot(matrix.T, matrix, precision=HI)
        poly = quintic_two * gram + quintic_three * jnp.dot(gram, gram, precision=HI)
        matrix = quintic_one * matrix + jnp.dot(matrix, poly, precision=HI)
    return matrix


def adam(coef_own, first_moment, second_moment):
    first = beta_one * first_moment + (1.0 - beta_one) * coef_own
    second = beta_two * second_moment + (1.0 - beta_two) * coef_own * coef_own
    direct_own = first / bias_one / (jnp.sqrt(second / bias_two) + adam_eps)
    return first, second, direct_own


def general(weight, basis, inputs, out_grads, first_moment, second_moment):
    shard_idx = lax.axis_index("shards")
    basis_now = basis[0]
    gradient = lax.psum(
        jnp.dot(inputs[0].T, out_grads[0], preferred_element_type=jnp.float32), "shards"
    )
    coeffs = jnp.dot(basis_now.T, gradient, precision=HI)
    rank_rows = first_moment.shape[1]
    coef_own = lax.dynamic_slice_in_dim(coeffs, shard_idx * rank_rows, rank_rows, 0)
    first, second, direct_own = adam(coef_own, first_moment[0], second_moment[0])
    direction = lax.all_gather(direct_own, "shards", axis=0, tiled=True)
    updated = weight[0] - step_rate * jnp.dot(basis_now, direction, precision=HI)
    subspace = lax.psum(jnp.dot(gradient, coeffs.T, precision=HI), "tensor")
    start_point = subspace / jnp.sqrt(jnp.sum(subspace * subspace) + norm_eps)
    return updated[None], quintic(start_point)[None], first[None], second[None]


F32, BF16 = jnp.float32, jnp.bfloat16
VMEM = pltpu.VMEM
PARTS = 2


def nn(a, b):
    return lax.dot_general(a, b, (((1,), (0,)), ((), ())), preferred_element_type=F32)


def nt(a, b):
    return lax.dot_general(a, b, (((1,), (1,)), ((), ())), preferred_element_type=F32)


def parts(x, n):
    out = []
    for i in range(n):
        out.append(x.astype(BF16))
        if i < n - 1:
            x = x - out[-1].astype(F32)
    return out


def left(dot, pieces, b):
    terms = [dot(p, b) for p in reversed(pieces)]
    return sum(terms[1:], terms[0])


def both(dot, a, b):
    return (dot(a[0], b[1]) + dot(a[1], b[0])) + dot(a[0], b[0])


def first_kernel(x_hbm, y_hbm, basis_hbm, c_ref, x_ref, y_ref, basis_ref, sems):
    n = sems.shape[0] - 2
    rows = basis_ref.shape[0] // n
    spans = [pl.ds(i * rows, rows) for i in range(n)]
    x_copy = pltpu.make_async_copy(x_hbm, x_ref, sems.at[n])
    y_copy = pltpu.make_async_copy(y_hbm, y_ref, sems.at[n + 1])
    copies = [
        pltpu.make_async_copy(basis_hbm.at[at, :], basis_ref.at[at, :], sems.at[i])
        for i, at in enumerate(spans)
    ]
    for copy in (x_copy, *copies, y_copy):
        copy.start()
    x_copy.wait()
    total = None
    for copy, at in zip(copies, spans):
        copy.wait()
        hi, lo = parts(basis_ref[at, :], 2)
        x = x_ref[:, at]
        term = nn(x, lo) + nn(x, hi)
        total = term if total is None else total + term
    y_copy.wait()
    c_ref[...] = left(nn, parts(total.T, PARTS), y_ref[...])


def own_kernel(x_ref, x32_ref, k_ref, xt_ref):
    x = x_ref[...]
    x32 = x.astype(F32)
    x32_ref[...] = x32
    for i, piece in enumerate(parts(nt(x, x), PARTS)):
        k_ref[i] = piece
    xt_ref[...] = x32.T.astype(BF16)


def other_kernel(x_ref, xo_ref, kox_ref, kxx_ref, xt_ref):
    x32 = x_ref[...]
    x = x32.astype(BF16)
    for a, ref in ((xo_ref[...], kox_ref), (x, kxx_ref)):
        for i, piece in enumerate(parts(nt(a, x), PARTS)):
            ref[i] = piece
    xt_ref[...] = x32.T.astype(BF16)


def moment_kernel(co_ref, cx_ref, y_ref, m_ref, v_ref, first_ref, second_ref, dir_ref, z_ref, c_ref):
    c = co_ref[...] + cx_ref[...]
    c_ref[...] = c
    z_ref[...] = left(nt, parts(c, PARTS), y_ref[...])
    rows = m_ref.shape[0]
    own = c_ref[pl.ds(pl.multiple_of(lax.axis_index("shards") * rows, rows), rows), :]
    first = beta_one * m_ref[...] + (1.0 - beta_one) * own
    second = beta_two * v_ref[...] + (1.0 - beta_two) * own * own
    first_ref[...] = first
    second_ref[...] = second
    dir_ref[...] = first / bias_one / (jnp.sqrt(second / bias_two) + adam_eps)


def add_kernel(a_ref, b_ref, o_ref):
    o_ref[...] = a_ref[...] + b_ref[...]


def weight_kernel(w_ref, basis_ref, do_ref, dx_ref, m_ref, v_ref,
                  o_ref, first_ref, second_ref, dir_ref, buf, sems):
    rows = do_ref.shape[0]
    copies = [
        pltpu.make_async_copy(m_ref, first_ref, sems.at[0]),
        pltpu.make_async_copy(v_ref, second_ref, sems.at[1]),
    ]
    for copy in copies:
        copy.start()
    shard = lax.axis_index("shards")
    for which, ref in ((shard, do_ref), (1 - shard, dx_ref)):
        for i, piece in enumerate(parts(ref[...], 2)):
            dir_ref[i, pl.ds(pl.multiple_of(which * rows, rows), rows), :] = piece
    direction = [dir_ref[0], dir_ref[1]]
    n = sems.shape[0] - 2
    rows = o_ref.shape[0] // n
    for i in range(n):
        at = pl.ds(i * rows, rows)
        step = both(nn, parts(basis_ref[at, :], 2), direction)
        buf[at, :] = w_ref[at, :] - step_rate * step
        copies.append(pltpu.make_async_copy(buf.at[at, :], o_ref.at[at, :], sems.at[2 + i]))
        copies[-1].start()
    for copy in copies:
        copy.wait()


def stacked(a, b):
    n = a[0].shape[0]
    terms = nn(jnp.concatenate(a, 0), b[0])
    return (terms[n:] + nn(a[0], b[1])) + terms[:n]


def gram_quintic(gram):
    n = gram.shape[0] // 2
    whole = lambda halves: [jnp.concatenate(h, 0) for h in zip(*halves)]
    rows = [gram[:n], gram[n:]]
    total = None
    for sweep in range(ITERS):
        g = [parts(h, 2) for h in rows]
        square = whole(g)
        poly = [quintic_two * h + quintic_three * stacked(p, square) for h, p in zip(rows, g)]
        p = whole([parts(h, 2) for h in poly])
        if total is None:
            r = lax.broadcasted_iota(jnp.int32, gram.shape, 0)
            c = lax.broadcasted_iota(jnp.int32, gram.shape, 1)
            first = jnp.where(r == c, quintic_one, 0.0)
            total = [first[:n] + poly[0], first[n:] + poly[1]]
            half = [quintic_one * h + stacked(q, p) for h, q in zip(rows, g)]
        elif sweep < ITERS - 1:
            steps = [stacked(whole((q, parts(t, 2))), p) for q, t in zip(g, total)]
            half = [quintic_one * h + step[:n] for h, step in zip(rows, steps)]
            total = [quintic_one * t + step[n:] for t, step in zip(total, steps)]
        else:
            total = [quintic_one * t + stacked(parts(t, 2), p) for t in total]
        if sweep < ITERS - 1:
            rows = [quintic_one * h + stacked(parts(h, 2), p) for h in half]
    return jnp.concatenate(total, 0)


def early_kernel(zo_ref, koo_ref, kox_ref, gram_ref, mixed_ref, zo2_ref):
    zo2 = parts(zo_ref[...], 2)
    gram_ref[...] = both(nt, parts(both(nn, zo2, [koo_ref[0], koo_ref[1]]), 2), zo2)
    mixed = parts(both(nn, zo2, [kox_ref[0], kox_ref[1]]), 2)
    for i in range(2):
        mixed_ref[i] = mixed[i]
        zo2_ref[i] = zo2[i]


def basis_kernel(gram_ref, mixed_ref, zo2_ref, zx_ref, kxx_ref, xto_ref, xtx_ref, o_ref, buf, sems):
    zo2, zx2 = [zo2_ref[0], zo2_ref[1]], parts(zx_ref[...], 2)
    cross = both(nt, [mixed_ref[0], mixed_ref[1]], zx2)
    gram = both(nt, parts(both(nn, zx2, [kxx_ref[0], kxx_ref[1]]), 2), zx2)
    gram = (gram_ref[...] + gram) + (cross + cross.T)
    r = lax.broadcasted_iota(jnp.int32, gram.shape, 0)
    c = lax.broadcasted_iota(jnp.int32, gram.shape, 1)
    trace = jnp.sum(jnp.where(r == c, gram, 0.0), keepdims=True)
    inverse = 1.0 / (trace + norm_eps)
    total = parts(gram_quintic(gram * inverse) * jnp.sqrt(inverse), 2)
    wo = parts(both(nn, total, zo2), 2)
    wx = parts(both(nn, total, zx2), 2)
    n = sems.shape[0]
    rows = o_ref.shape[0] // n
    copies = []
    for i in range(n):
        at = pl.ds(i * rows, rows)
        xo, xx = xto_ref[at, :], xtx_ref[at, :]
        buf[at, :] = (nt(xo, wo[1]) + nt(xo, wo[0])) + (nt(xx, wx[1]) + nt(xx, wx[0]))
        copies.append(pltpu.make_async_copy(buf.at[at, :], o_ref.at[at, :], sems.at[i]))
        copies[-1].start()
    for copy in copies:
        copy.wait()


def call(kernel, outs, ins, scratch=(), cost=0, name=None, **more):
    return pl.pallas_call(
        kernel,
        out_shape=outs,
        scratch_shapes=scratch,
        name=name,
        cost_estimate=pl.CostEstimate(flops=cost, bytes_accessed=4 << 20, transcendentals=0),
        compiler_params=pltpu.CompilerParams(vmem_limit_bytes=20 << 20),
        **more,
    )(*ins)


def paired(weight, basis, inputs, out_grads, first_moment, second_moment):
    tokens, width = inputs.shape[1:]
    features, rank = out_grads.shape[2], basis.shape[2]
    rows = first_moment.shape[1]
    swap = lambda a: lax.ppermute(a, "shards", [(0, 1), (1, 0)])

    def send(a, masks):
        pairs = [(s * 4 + t, s * 4 + (t ^ masks[s])) for s in range(2) for t in range(4)]
        return lax.ppermute(a, ("shards", "tensor"), pairs)

    sds = jax.ShapeDtypeStruct
    vm = pl.BlockSpec(memory_space=VMEM)
    def run(kernel, outs, ins, cost, scratch=(), in_specs=None, out_specs=None, name=None):
        return call(kernel, outs, ins, scratch, cost, name,
                    in_specs=in_specs or [vm] * len(ins),
                    out_specs=out_specs or jax.tree.map(lambda _: vm, outs))

    after = lax.optimization_barrier
    far = pl.BlockSpec(memory_space=pl.ANY)
    hbm = [pltpu.with_memory_space_constraint(a[0], pltpu.HBM) for a in (inputs, out_grads, basis)]
    square = (rank, features)
    c_own, x_bf, y_own, basis_now = run(
        first_kernel,
        (VMEM(square, F32), VMEM((tokens, width), BF16), VMEM((tokens, features), BF16), VMEM((width, rank), F32)),
        hbm, 100,
        scratch=[pltpu.SemaphoreType.DMA((3,))],
        in_specs=[pl.BlockSpec(memory_space=pltpu.HBM)] * 3, name="coefficients",
    )
    c_oth = swap(c_own)
    kept = VMEM((PARTS, tokens, tokens), BF16)
    turned = VMEM((width, tokens), BF16)
    x_own, koo, xto = run(own_kernel, (VMEM((tokens, width), F32), kept, turned), [x_bf], 100, name="own")
    koo, c_oth = after((koo, c_oth))
    zt = VMEM((rank, tokens), F32)
    small = VMEM((rows, features), F32)
    first, second, d_own, z_one = run(
        moment_kernel, (small, small, small, zt),
        [c_own, c_oth, y_own, first_moment[0], second_moment[0]], 100,
        scratch=[VMEM(square, F32)], name="moments",
    )
    z_got = send(z_one, (1, 2))
    x_own, d_own = after((x_own, d_own))
    x_oth = swap(x_own)
    kox, kxx, xtx = run(
        other_kernel, (kept, kept, turned), [x_oth, x_bf], 100, name="other"
    )
    z_got, kxx = after((z_got, kxx))
    z_two = run(add_kernel, zt, [z_one, z_got], 100, name="add1")
    z_got = send(z_two, (2, 1))
    d_own, z_two = after((d_own, z_two))
    d_oth = swap(d_own)
    updated, first, second = run(
        weight_kernel, (sds(weight.shape[1:], F32), sds(first.shape, F32), sds(second.shape, F32)),
        [weight[0], basis_now, d_own, d_oth, first, second], 100,
        scratch=[VMEM((2, rank, features), BF16), VMEM((width, features), F32), pltpu.SemaphoreType.DMA((6,))],
        out_specs=(far, far, far), name="weights",
    )
    z_got, updated = after((z_got, updated))
    z_own = run(add_kernel, zt, [z_two, z_got], 100, name="add2")
    z_oth = swap(z_own)
    gram, mixed, zo2 = run(
        early_kernel, (VMEM((rank, rank), F32), VMEM((2, rank, tokens), BF16), VMEM((2, rank, tokens), BF16)),
        [z_own, koo, kox], 100, name="early",
    )
    z_oth, gram = after((z_oth, gram))
    refreshed = run(
        basis_kernel, sds((width, rank), F32),
        [gram, mixed, zo2, z_oth, kxx, xto, xtx], 100,
        scratch=[VMEM((width, rank), F32), pltpu.SemaphoreType.DMA((4,))],
        out_specs=far, name="basis",
    )
    return updated[None], refreshed[None], first[None], second[None]


def solution(mesh):
    placed = (
        P("sections", None, "tensor"),
        P("sections", None, None),
        P("sections", "shards", None),
        P("sections", "shards", "tensor"),
        P("sections", "shards", "tensor"),
        P("sections", "shards", "tensor"),
    )
    fits = mesh.shape["shards"] == 2 and mesh.shape["tensor"] == 4
    return jax.shard_map(
        paired if fits else general,
        mesh=mesh,
        in_specs=placed,
        out_specs=(
            P("sections", None, "tensor"),
            P("sections", None, None),
            P("sections", "shards", "tensor"),
            P("sections", "shards", "tensor"),
        ),
        check_vma=False,
    )
```

```python
import jax
import jax.numpy as jnp
from jax import lax
from jax.experimental import pallas as pl
from jax.experimental.pallas import tpu as pltpu
from jax.sharding import PartitionSpec as P

ITERS = 5


beta_one = 0.9
beta_two = 0.99
bias_one = 1.0 - 0.9**10
bias_two = 1.0 - 0.99**10
adam_eps = 1e-08
norm_eps = 1e-06
step_rate = 0.2
quintic_one = 3.4445
quintic_two = -4.775
quintic_three = 2.0315

HI = lax.Precision.HIGHEST


def quintic(matrix):
    for sweep in range(ITERS):
        gram = jnp.dot(matrix.T, matrix, precision=HI)
        poly = quintic_two * gram + quintic_three * jnp.dot(gram, gram, precision=HI)
        matrix = quintic_one * matrix + jnp.dot(matrix, poly, precision=HI)
    return matrix


def adam(coef_own, first_moment, second_moment):
    first = beta_one * first_moment + (1.0 - beta_one) * coef_own
    second = beta_two * second_moment + (1.0 - beta_two) * coef_own * coef_own
    direct_own = first / bias_one / (jnp.sqrt(second / bias_two) + adam_eps)
    return first, second, direct_own


def general(weight, basis, inputs, out_grads, first_moment, second_moment):
    shard_idx = lax.axis_index("shards")
    basis_now = basis[0]
    gradient = lax.psum(
        jnp.dot(inputs[0].T, out_grads[0], preferred_element_type=jnp.float32), "shards"
    )
    coeffs = jnp.dot(basis_now.T, gradient, precision=HI)
    rank_rows = first_moment.shape[1]
    coef_own = lax.dynamic_slice_in_dim(coeffs, shard_idx * rank_rows, rank_rows, 0)
    first, second, direct_own = adam(coef_own, first_moment[0], second_moment[0])
    direction = lax.all_gather(direct_own, "shards", axis=0, tiled=True)
    updated = weight[0] - step_rate * jnp.dot(basis_now, direction, precision=HI)
    subspace = lax.psum(jnp.dot(gradient, coeffs.T, precision=HI), "tensor")
    start_point = subspace / jnp.sqrt(jnp.sum(subspace * subspace) + norm_eps)
    return updated[None], quintic(start_point)[None], first[None], second[None]


F32, BF16 = jnp.float32, jnp.bfloat16
VMEM = pltpu.VMEM
PARTS = 2


def nn(a, b):
    return lax.dot_general(a, b, (((1,), (0,)), ((), ())), preferred_element_type=F32)


def nt(a, b):
    return lax.dot_general(a, b, (((1,), (1,)), ((), ())), preferred_element_type=F32)


def parts(x, n):
    out = []
    for i in range(n):
        out.append(x.astype(BF16))
        if i < n - 1:
            x = x - out[-1].astype(F32)
    return out


def left(dot, pieces, b):
    terms = [dot(p, b) for p in reversed(pieces)]
    return sum(terms[1:], terms[0])


def both(dot, a, b):
    return (dot(a[0], b[1]) + dot(a[1], b[0])) + dot(a[0], b[0])


def first_kernel(x_hbm, y_hbm, basis_hbm, c_ref, x_ref, y_ref, basis_ref, sems):
    n = sems.shape[0] - 2
    rows = basis_ref.shape[0] // n
    spans = [pl.ds(i * rows, rows) for i in range(n)]
    x_copy = pltpu.make_async_copy(x_hbm, x_ref, sems.at[n])
    y_copy = pltpu.make_async_copy(y_hbm, y_ref, sems.at[n + 1])
    copies = [
        pltpu.make_async_copy(basis_hbm.at[at, :], basis_ref.at[at, :], sems.at[i])
        for i, at in enumerate(spans)
    ]
    for copy in (x_copy, *copies, y_copy):
        copy.start()
    x_copy.wait()
    total = None
    for copy, at in zip(copies, spans):
        copy.wait()
        hi, lo = parts(basis_ref[at, :], 2)
        x = x_ref[:, at]
        term = nn(x, lo) + nn(x, hi)
        total = term if total is None else total + term
    y_copy.wait()
    c_ref[...] = left(nn, parts(total.T, PARTS), y_ref[...])


def own_kernel(x_ref, x32_ref, k_ref, xt_ref):
    x = x_ref[...]
    x32 = x.astype(F32)
    x32_ref[...] = x32
    for i, piece in enumerate(parts(nt(x, x), PARTS)):
        k_ref[i] = piece
    xt_ref[...] = x32.T.astype(BF16)


def other_kernel(x_ref, xo_ref, kox_ref, kxx_ref, xt_ref):
    x32 = x_ref[...]
    x = x32.astype(BF16)
    for a, ref in ((xo_ref[...], kox_ref), (x, kxx_ref)):
        for i, piece in enumerate(parts(nt(a, x), PARTS)):
            ref[i] = piece
    xt_ref[...] = x32.T.astype(BF16)


def share_kernel(co_ref, cx_ref, y_ref, c_ref, z_ref):
    c = co_ref[...] + cx_ref[...]
    c_ref[...] = c
    z_ref[...] = left(nt, parts(c, PARTS), y_ref[...])


def moment_kernel(c_ref, m_ref, v_ref, first_ref, second_ref, dir_ref):
    rows = m_ref.shape[0]
    own = c_ref[pl.ds(pl.multiple_of(lax.axis_index("shards") * rows, rows), rows), :]
    first = beta_one * m_ref[...] + (1.0 - beta_one) * own
    second = beta_two * v_ref[...] + (1.0 - beta_two) * own * own
    first_ref[...] = first
    second_ref[...] = second
    dir_ref[...] = first / bias_one / (jnp.sqrt(second / bias_two) + adam_eps)


def add_kernel(a_ref, b_ref, o_ref):
    o_ref[...] = a_ref[...] + b_ref[...]


def weight_kernel(w_ref, basis_ref, do_ref, dx_ref, m_ref, v_ref,
                  o_ref, first_ref, second_ref, dir_ref, buf, sems):
    rows = do_ref.shape[0]
    copies = [
        pltpu.make_async_copy(m_ref, first_ref, sems.at[0]),
        pltpu.make_async_copy(v_ref, second_ref, sems.at[1]),
    ]
    for copy in copies:
        copy.start()
    shard = lax.axis_index("shards")
    for which, ref in ((shard, do_ref), (1 - shard, dx_ref)):
        for i, piece in enumerate(parts(ref[...], 2)):
            dir_ref[i, pl.ds(pl.multiple_of(which * rows, rows), rows), :] = piece
    direction = [dir_ref[0], dir_ref[1]]
    n = sems.shape[0] - 2
    rows = o_ref.shape[0] // n
    for i in range(n):
        at = pl.ds(i * rows, rows)
        step = both(nn, parts(basis_ref[at, :], 2), direction)
        buf[at, :] = w_ref[at, :] - step_rate * step
        copies.append(pltpu.make_async_copy(buf.at[at, :], o_ref.at[at, :], sems.at[2 + i]))
        copies[-1].start()
    for copy in copies:
        copy.wait()


def stacked(a, b):
    n = a[0].shape[0]
    terms = nn(jnp.concatenate(a, 0), b[0])
    return (terms[n:] + nn(a[0], b[1])) + terms[:n]


def gram_quintic(gram):
    n = gram.shape[0] // 2
    whole = lambda halves: [jnp.concatenate(h, 0) for h in zip(*halves)]
    rows = [gram[:n], gram[n:]]
    total = None
    for sweep in range(ITERS):
        g = [parts(h, 2) for h in rows]
        square = whole(g)
        poly = [quintic_two * h + quintic_three * stacked(p, square) for h, p in zip(rows, g)]
        p = whole([parts(h, 2) for h in poly])
        if total is None:
            r = lax.broadcasted_iota(jnp.int32, gram.shape, 0)
            c = lax.broadcasted_iota(jnp.int32, gram.shape, 1)
            first = jnp.where(r == c, quintic_one, 0.0)
            total = [first[:n] + poly[0], first[n:] + poly[1]]
            half = [quintic_one * h + stacked(q, p) for h, q in zip(rows, g)]
        elif sweep < ITERS - 1:
            steps = [stacked(whole((q, parts(t, 2))), p) for q, t in zip(g, total)]
            half = [quintic_one * h + step[:n] for h, step in zip(rows, steps)]
            total = [quintic_one * t + step[n:] for t, step in zip(total, steps)]
        else:
            total = [quintic_one * t + stacked(parts(t, 2), p) for t in total]
        if sweep < ITERS - 1:
            rows = [quintic_one * h + stacked(parts(h, 2), p) for h in half]
    return jnp.concatenate(total, 0)


def early_kernel(zo_ref, koo_ref, kox_ref, gram_ref, mixed_ref, zo2_ref):
    zo2 = parts(zo_ref[...], 2)
    gram_ref[...] = both(nt, parts(both(nn, zo2, [koo_ref[0], koo_ref[1]]), 2), zo2)
    mixed = parts(both(nn, zo2, [kox_ref[0], kox_ref[1]]), 2)
    for i in range(2):
        mixed_ref[i] = mixed[i]
        zo2_ref[i] = zo2[i]


def basis_kernel(gram_ref, mixed_ref, zo2_ref, zx_ref, kxx_ref, xto_ref, xtx_ref, o_ref, buf, sems):
    zo2, zx2 = [zo2_ref[0], zo2_ref[1]], parts(zx_ref[...], 2)
    cross = both(nt, [mixed_ref[0], mixed_ref[1]], zx2)
    gram = both(nt, parts(both(nn, zx2, [kxx_ref[0], kxx_ref[1]]), 2), zx2)
    gram = (gram_ref[...] + gram) + (cross + cross.T)
    r = lax.broadcasted_iota(jnp.int32, gram.shape, 0)
    c = lax.broadcasted_iota(jnp.int32, gram.shape, 1)
    trace = jnp.sum(jnp.where(r == c, gram, 0.0), keepdims=True)
    inverse = 1.0 / (trace + norm_eps)
    total = parts(gram_quintic(gram * inverse) * jnp.sqrt(inverse), 2)
    wo = parts(both(nn, total, zo2), 2)
    wx = parts(both(nn, total, zx2), 2)
    n = sems.shape[0]
    rows = o_ref.shape[0] // n
    copies = []
    for i in range(n):
        at = pl.ds(i * rows, rows)
        xo, xx = xto_ref[at, :], xtx_ref[at, :]
        buf[at, :] = (nt(xo, wo[1]) + nt(xo, wo[0])) + (nt(xx, wx[1]) + nt(xx, wx[0]))
        copies.append(pltpu.make_async_copy(buf.at[at, :], o_ref.at[at, :], sems.at[i]))
        copies[-1].start()
    for copy in copies:
        copy.wait()


def call(kernel, outs, ins, scratch=(), cost=0, name=None, **more):
    return pl.pallas_call(
        kernel,
        out_shape=outs,
        scratch_shapes=scratch,
        name=name,
        cost_estimate=pl.CostEstimate(flops=cost, bytes_accessed=4 << 20, transcendentals=0),
        compiler_params=pltpu.CompilerParams(vmem_limit_bytes=20 << 20),
        **more,
    )(*ins)


def paired(weight, basis, inputs, out_grads, first_moment, second_moment):
    tokens, width = inputs.shape[1:]
    features, rank = out_grads.shape[2], basis.shape[2]
    rows = first_moment.shape[1]
    swap = lambda a: lax.ppermute(a, "shards", [(0, 1), (1, 0)])

    def send(a, masks):
        pairs = [(s * 4 + t, s * 4 + (t ^ masks[s])) for s in range(2) for t in range(4)]
        return lax.ppermute(a, ("shards", "tensor"), pairs)

    sds = jax.ShapeDtypeStruct
    vm = pl.BlockSpec(memory_space=VMEM)
    def run(kernel, outs, ins, cost, scratch=(), in_specs=None, out_specs=None, name=None):
        return call(kernel, outs, ins, scratch, cost, name,
                    in_specs=in_specs or [vm] * len(ins),
                    out_specs=out_specs or jax.tree.map(lambda _: vm, outs))

    after = lax.optimization_barrier
    far = pl.BlockSpec(memory_space=pl.ANY)
    hbm = [pltpu.with_memory_space_constraint(a[0], pltpu.HBM) for a in (inputs, out_grads, basis)]
    square = (rank, features)
    c_own, x_bf, y_own, basis_now = run(
        first_kernel,
        (VMEM(square, F32), VMEM((tokens, width), BF16), VMEM((tokens, features), BF16), VMEM((width, rank), F32)),
        hbm, 100,
        scratch=[pltpu.SemaphoreType.DMA((3,))],
        in_specs=[pl.BlockSpec(memory_space=pltpu.HBM)] * 3, name="coefficients",
    )
    c_oth = swap(c_own)
    kept = VMEM((PARTS, tokens, tokens), BF16)
    turned = VMEM((width, tokens), BF16)
    x_own, koo, xto = run(own_kernel, (VMEM((tokens, width), F32), kept, turned), [x_bf], 100, name="own")
    koo, c_oth = after((koo, c_oth))
    zt = VMEM((rank, tokens), F32)
    small = VMEM((rows, features), F32)
    coeffs, z_one = run(share_kernel, (VMEM(square, F32), zt), [c_own, c_oth, y_own], 100, name="share")
    z_got = send(z_one, (1, 2))
    x_own, coeffs = after((x_own, coeffs))
    x_oth = swap(x_own)
    kox, kxx, xtx = run(
        other_kernel, (kept, kept, turned), [x_oth, x_bf], 100, name="other"
    )
    coeffs, kxx = after((coeffs, kxx))
    first, second, d_own = run(
        moment_kernel, (small, small, small), [coeffs, first_moment[0], second_moment[0]], 100, name="moments"
    )
    z_got, d_own = after((z_got, d_own))
    z_two = run(add_kernel, zt, [z_one, z_got], 100, name="add1")
    z_got = send(z_two, (2, 1))
    d_own, z_two = after((d_own, z_two))
    d_oth = swap(d_own)
    updated, first, second = run(
        weight_kernel, (sds(weight.shape[1:], F32), sds(first.shape, F32), sds(second.shape, F32)),
        [weight[0], basis_now, d_own, d_oth, first, second], 100,
        scratch=[VMEM((2, rank, features), BF16), VMEM((width, features), F32), pltpu.SemaphoreType.DMA((6,))],
        out_specs=(far, far, far), name="weights",
    )
    z_got, updated = after((z_got, updated))
    z_own = run(add_kernel, zt, [z_two, z_got], 100, name="add2")
    z_oth = swap(z_own)
    gram, mixed, zo2 = run(
        early_kernel, (VMEM((rank, rank), F32), VMEM((2, rank, tokens), BF16), VMEM((2, rank, tokens), BF16)),
        [z_own, koo, kox], 100, name="early",
    )
    z_oth, gram = after((z_oth, gram))
    refreshed = run(
        basis_kernel, sds((width, rank), F32),
        [gram, mixed, zo2, z_oth, kxx, xto, xtx], 100,
        scratch=[VMEM((width, rank), F32), pltpu.SemaphoreType.DMA((4,))],
        out_specs=far, name="basis",
    )
    return updated[None], refreshed[None], first[None], second[None]


def solution(mesh):
    placed = (
        P("sections", None, "tensor"),
        P("sections", None, None),
        P("sections", "shards", None),
        P("sections", "shards", "tensor"),
        P("sections", "shards", "tensor"),
        P("sections", "shards", "tensor"),
    )
    fits = mesh.shape["shards"] == 2 and mesh.shape["tensor"] == 4
    return jax.shard_map(
        paired if fits else general,
        mesh=mesh,
        in_specs=placed,
        out_specs=(
            P("sections", None, "tensor"),
            P("sections", None, None),
            P("sections", "shards", "tensor"),
            P("sections", "shards", "tensor"),
        ),
        check_vma=False,
    )
```

```python
import jax
import jax.numpy as jnp
from jax import lax
from jax.experimental import pallas as pl
from jax.experimental.pallas import tpu as pltpu
from jax.sharding import PartitionSpec as P

ITERS = 5


beta_one = 0.9
beta_two = 0.99
bias_one = 1.0 - 0.9**10
bias_two = 1.0 - 0.99**10
adam_eps = 1e-08
norm_eps = 1e-06
step_rate = 0.2
quintic_one = 3.4445
quintic_two = -4.775
quintic_three = 2.0315

HI = lax.Precision.HIGHEST


def quintic(matrix):
    for sweep in range(ITERS):
        gram = jnp.dot(matrix.T, matrix, precision=HI)
        poly = quintic_two * gram + quintic_three * jnp.dot(gram, gram, precision=HI)
        matrix = quintic_one * matrix + jnp.dot(matrix, poly, precision=HI)
    return matrix


def adam(coef_own, first_moment, second_moment):
    first = beta_one * first_moment + (1.0 - beta_one) * coef_own
    second = beta_two * second_moment + (1.0 - beta_two) * coef_own * coef_own
    direct_own = first / bias_one / (jnp.sqrt(second / bias_two) + adam_eps)
    return first, second, direct_own


def general(weight, basis, inputs, out_grads, first_moment, second_moment):
    shard_idx = lax.axis_index("shards")
    basis_now = basis[0]
    gradient = lax.psum(
        jnp.dot(inputs[0].T, out_grads[0], preferred_element_type=jnp.float32), "shards"
    )
    coeffs = jnp.dot(basis_now.T, gradient, precision=HI)
    rank_rows = first_moment.shape[1]
    coef_own = lax.dynamic_slice_in_dim(coeffs, shard_idx * rank_rows, rank_rows, 0)
    first, second, direct_own = adam(coef_own, first_moment[0], second_moment[0])
    direction = lax.all_gather(direct_own, "shards", axis=0, tiled=True)
    updated = weight[0] - step_rate * jnp.dot(basis_now, direction, precision=HI)
    subspace = lax.psum(jnp.dot(gradient, coeffs.T, precision=HI), "tensor")
    start_point = subspace / jnp.sqrt(jnp.sum(subspace * subspace) + norm_eps)
    return updated[None], quintic(start_point)[None], first[None], second[None]


F32, BF16 = jnp.float32, jnp.bfloat16
VMEM = pltpu.VMEM
PARTS = 2


def nn(a, b):
    return lax.dot_general(a, b, (((1,), (0,)), ((), ())), preferred_element_type=F32)


def nt(a, b):
    return lax.dot_general(a, b, (((1,), (1,)), ((), ())), preferred_element_type=F32)


def parts(x, n):
    out = []
    for i in range(n):
        out.append(x.astype(BF16))
        if i < n - 1:
            x = x - out[-1].astype(F32)
    return out


def left(dot, pieces, b):
    terms = [dot(p, b) for p in reversed(pieces)]
    return sum(terms[1:], terms[0])


def both(dot, a, b):
    return (dot(a[0], b[1]) + dot(a[1], b[0])) + dot(a[0], b[0])


def first_kernel(x_hbm, y_hbm, basis_hbm, c_ref, x_ref, y_ref, basis_ref, sems):
    n = sems.shape[0] - 2
    rows = basis_ref.shape[0] // n
    spans = [pl.ds(i * rows, rows) for i in range(n)]
    x_copy = pltpu.make_async_copy(x_hbm, x_ref, sems.at[n])
    y_copy = pltpu.make_async_copy(y_hbm, y_ref, sems.at[n + 1])
    copies = [
        pltpu.make_async_copy(basis_hbm.at[at, :], basis_ref.at[at, :], sems.at[i])
        for i, at in enumerate(spans)
    ]
    for copy in (x_copy, *copies, y_copy):
        copy.start()
    x_copy.wait()
    total = None
    for copy, at in zip(copies, spans):
        copy.wait()
        hi, lo = parts(basis_ref[at, :], 2)
        x = x_ref[:, at]
        term = nn(x, lo) + nn(x, hi)
        total = term if total is None else total + term
    y_copy.wait()
    c_ref[...] = left(nn, parts(total.T, PARTS), y_ref[...])


def own_kernel(x_ref, x32_ref, k_ref, xt_ref):
    x = x_ref[...]
    x32 = x.astype(F32)
    x32_ref[...] = x32
    for i, piece in enumerate(parts(nt(x, x), PARTS)):
        k_ref[i] = piece
    xt_ref[...] = x32.T.astype(BF16)


def other_kernel(x_ref, xo_ref, kox_ref, kxx_ref, xt_ref):
    x32 = x_ref[...]
    x = x32.astype(BF16)
    for a, ref in ((xo_ref[...], kox_ref), (x, kxx_ref)):
        for i, piece in enumerate(parts(nt(a, x), PARTS)):
            ref[i] = piece
    xt_ref[...] = x32.T.astype(BF16)


def moment_kernel(co_ref, cx_ref, y_ref, m_ref, v_ref, first_ref, second_ref, dir_ref, z_ref, c_ref):
    c = co_ref[...] + cx_ref[...]
    c_ref[...] = c
    z_ref[...] = left(nt, parts(c, PARTS), y_ref[...])
    rows = m_ref.shape[0]
    own = c_ref[pl.ds(pl.multiple_of(lax.axis_index("shards") * rows, rows), rows), :]
    first = beta_one * m_ref[...] + (1.0 - beta_one) * own
    second = beta_two * v_ref[...] + (1.0 - beta_two) * own * own
    first_ref[...] = first
    second_ref[...] = second
    dir_ref[...] = first / bias_one / (jnp.sqrt(second / bias_two) + adam_eps)


def add_kernel(a_ref, b_ref, o_ref):
    o_ref[...] = a_ref[...] + b_ref[...]


def weight_kernel(w_ref, basis_ref, do_ref, dx_ref, m_ref, v_ref,
                  o_ref, first_ref, second_ref, dir_ref, buf, sems):
    rows = do_ref.shape[0]
    copies = [
        pltpu.make_async_copy(m_ref, first_ref, sems.at[0]),
        pltpu.make_async_copy(v_ref, second_ref, sems.at[1]),
    ]
    for copy in copies:
        copy.start()
    shard = lax.axis_index("shards")
    for which, ref in ((shard, do_ref), (1 - shard, dx_ref)):
        for i, piece in enumerate(parts(ref[...], 2)):
            dir_ref[i, pl.ds(pl.multiple_of(which * rows, rows), rows), :] = piece
    direction = [dir_ref[0], dir_ref[1]]
    n = sems.shape[0] - 2
    rows = o_ref.shape[0] // n
    for i in range(n):
        at = pl.ds(i * rows, rows)
        step = both(nn, parts(basis_ref[at, :], 2), direction)
        buf[at, :] = w_ref[at, :] - step_rate * step
        copies.append(pltpu.make_async_copy(buf.at[at, :], o_ref.at[at, :], sems.at[2 + i]))
        copies[-1].start()
    for copy in copies:
        copy.wait()


def stacked(a, b):
    n = a[0].shape[0]
    terms = nn(jnp.concatenate(a, 0), b[0])
    return (terms[n:] + nn(a[0], b[1])) + terms[:n]


def gram_quintic(gram):
    n = gram.shape[0] // 2
    whole = lambda halves: [jnp.concatenate(h, 0) for h in zip(*halves)]
    rows = [gram[:n], gram[n:]]
    total = None
    for sweep in range(ITERS):
        g = [parts(h, 2) for h in rows]
        square = whole(g)
        poly = [quintic_two * h + quintic_three * stacked(p, square) for h, p in zip(rows, g)]
        p = whole([parts(h, 2) for h in poly])
        if total is None:
            r = lax.broadcasted_iota(jnp.int32, gram.shape, 0)
            c = lax.broadcasted_iota(jnp.int32, gram.shape, 1)
            first = jnp.where(r == c, quintic_one, 0.0)
            total = [first[:n] + poly[0], first[n:] + poly[1]]
            half = [quintic_one * h + stacked(q, p) for h, q in zip(rows, g)]
        elif sweep < ITERS - 1:
            steps = [stacked(whole((q, parts(t, 2))), p) for q, t in zip(g, total)]
            half = [quintic_one * h + step[:n] for h, step in zip(rows, steps)]
            total = [quintic_one * t + step[n:] for t, step in zip(total, steps)]
        else:
            total = [quintic_one * t + stacked(parts(t, 2), p) for t in total]
        if sweep < ITERS - 1:
            rows = [quintic_one * h + stacked(parts(h, 2), p) for h in half]
    return jnp.concatenate(total, 0)


def early_kernel(zo_ref, koo_ref, kox_ref, gram_ref, mixed_ref, zo2_ref):
    zo2 = parts(zo_ref[...], 2)
    gram_ref[...] = both(nt, parts(both(nn, zo2, [koo_ref[0], koo_ref[1]]), 2), zo2)
    mixed = parts(both(nn, zo2, [kox_ref[0], kox_ref[1]]), 2)
    for i in range(2):
        mixed_ref[i] = mixed[i]
        zo2_ref[i] = zo2[i]


def basis_kernel(gram_ref, mixed_ref, zo2_ref, zx_ref, kxx_ref, xto_ref, xtx_ref, o_ref, buf, sems):
    zo2, zx2 = [zo2_ref[0], zo2_ref[1]], parts(zx_ref[...], 2)
    cross = both(nt, [mixed_ref[0], mixed_ref[1]], zx2)
    gram = both(nt, parts(both(nn, zx2, [kxx_ref[0], kxx_ref[1]]), 2), zx2)
    gram = (gram_ref[...] + gram) + (cross + cross.T)
    r = lax.broadcasted_iota(jnp.int32, gram.shape, 0)
    c = lax.broadcasted_iota(jnp.int32, gram.shape, 1)
    trace = jnp.sum(jnp.where(r == c, gram, 0.0), keepdims=True)
    inverse = 1.0 / (trace + norm_eps)
    total = parts(gram_quintic(gram * inverse) * jnp.sqrt(inverse), 2)
    wo = parts(both(nn, total, zo2), 2)
    wx = parts(both(nn, total, zx2), 2)
    n = sems.shape[0]
    rows = o_ref.shape[0] // n
    copies = []
    for i in range(n):
        at = pl.ds(i * rows, rows)
        xo, xx = xto_ref[at, :], xtx_ref[at, :]
        buf[at, :] = (nt(xo, wo[1]) + nt(xo, wo[0])) + (nt(xx, wx[1]) + nt(xx, wx[0]))
        copies.append(pltpu.make_async_copy(buf.at[at, :], o_ref.at[at, :], sems.at[i]))
        copies[-1].start()
    for copy in copies:
        copy.wait()


def call(kernel, outs, ins, scratch=(), cost=0, name=None, **more):
    return pl.pallas_call(
        kernel,
        out_shape=outs,
        scratch_shapes=scratch,
        name=name,
        cost_estimate=pl.CostEstimate(flops=cost, bytes_accessed=4 << 20, transcendentals=0),
        compiler_params=pltpu.CompilerParams(vmem_limit_bytes=20 << 20),
        **more,
    )(*ins)


def paired(weight, basis, inputs, out_grads, first_moment, second_moment):
    tokens, width = inputs.shape[1:]
    features, rank = out_grads.shape[2], basis.shape[2]
    rows = first_moment.shape[1]
    swap = lambda a: lax.ppermute(a, "shards", [(0, 1), (1, 0)])

    def send(a, masks):
        pairs = [(s * 4 + t, s * 4 + (t ^ masks[s])) for s in range(2) for t in range(4)]
        return lax.ppermute(a, ("shards", "tensor"), pairs)

    sds = jax.ShapeDtypeStruct
    vm = pl.BlockSpec(memory_space=VMEM)
    def run(kernel, outs, ins, cost, scratch=(), in_specs=None, out_specs=None, name=None):
        return call(kernel, outs, ins, scratch, cost, name,
                    in_specs=in_specs or [vm] * len(ins),
                    out_specs=out_specs or jax.tree.map(lambda _: vm, outs))

    after = lax.optimization_barrier
    far = pl.BlockSpec(memory_space=pl.ANY)
    hbm = [pltpu.with_memory_space_constraint(a[0], pltpu.HBM) for a in (inputs, out_grads, basis)]
    square = (rank, features)
    c_own, x_bf, y_own, basis_now = run(
        first_kernel,
        (VMEM(square, F32), VMEM((tokens, width), BF16), VMEM((tokens, features), BF16), VMEM((width, rank), F32)),
        hbm, 100,
        scratch=[pltpu.SemaphoreType.DMA((3,))],
        in_specs=[pl.BlockSpec(memory_space=pltpu.HBM)] * 3, name="coefficients",
    )
    c_oth = swap(c_own)
    kept = VMEM((PARTS, tokens, tokens), BF16)
    turned = VMEM((width, tokens), BF16)
    x_own, koo, xto = run(own_kernel, (VMEM((tokens, width), F32), kept, turned), [x_bf], 100, name="own")
    koo, c_oth = after((koo, c_oth))
    zt = VMEM((rank, tokens), F32)
    small = VMEM((rows, features), F32)
    first, second, d_own, z_one = run(
        moment_kernel, (small, small, small, zt),
        [c_own, c_oth, y_own, first_moment[0], second_moment[0]], 100,
        scratch=[VMEM(square, F32)], name="moments",
    )
    z_got = send(z_one, (1, 2))
    z_two = run(add_kernel, zt, [z_one, z_got], 100, name="add1")
    z_got = send(z_two, (2, 1))
    x_own, d_own, z_two = after((x_own, d_own, z_two))
    d_oth = swap(d_own)
    x_oth = swap(x_own)
    kox, kxx, xtx = run(
        other_kernel, (kept, kept, turned), [x_oth, x_bf], 100, name="other"
    )
    d_oth, kxx = after((d_oth, kxx))
    updated, first, second = run(
        weight_kernel, (sds(weight.shape[1:], F32), sds(first.shape, F32), sds(second.shape, F32)),
        [weight[0], basis_now, d_own, d_oth, first, second], 100,
        scratch=[VMEM((2, rank, features), BF16), VMEM((width, features), F32), pltpu.SemaphoreType.DMA((6,))],
        out_specs=(far, far, far), name="weights",
    )
    z_got, updated = after((z_got, updated))
    z_own = run(add_kernel, zt, [z_two, z_got], 100, name="add2")
    z_oth = swap(z_own)
    gram, mixed, zo2 = run(
        early_kernel, (VMEM((rank, rank), F32), VMEM((2, rank, tokens), BF16), VMEM((2, rank, tokens), BF16)),
        [z_own, koo, kox], 100, name="early",
    )
    z_oth, gram = after((z_oth, gram))
    refreshed = run(
        basis_kernel, sds((width, rank), F32),
        [gram, mixed, zo2, z_oth, kxx, xto, xtx], 100,
        scratch=[VMEM((width, rank), F32), pltpu.SemaphoreType.DMA((4,))],
        out_specs=far, name="basis",
    )
    return updated[None], refreshed[None], first[None], second[None]


def solution(mesh):
    placed = (
        P("sections", None, "tensor"),
        P("sections", None, None),
        P("sections", "shards", None),
        P("sections", "shards", "tensor"),
        P("sections", "shards", "tensor"),
        P("sections", "shards", "tensor"),
    )
    fits = mesh.shape["shards"] == 2 and mesh.shape["tensor"] == 4
    return jax.shard_map(
        paired if fits else general,
        mesh=mesh,
        in_specs=placed,
        out_specs=(
            P("sections", None, "tensor"),
            P("sections", None, None),
            P("sections", "shards", "tensor"),
            P("sections", "shards", "tensor"),
        ),
        check_vma=False,
    )
```
